32 devices in a mesh: wide: 8 (over y, x, core), narrow: 4 (over z).
Axes of the slice: x: 2, y: 2, z: 4, core: 2. Of those that a mesh axis runs over, the one named last changes fastest.
Arguments:
- query_act: bfloat16 [64, 16384], P(None, 'wide'), may hold values from -6 to 6
- query_grad: bfloat16 [64, 16384], P(None, 'narrow'), may hold values from -6 to 6
- act_basis: bfloat16 [16384, 16384], P('wide', 'narrow'), may hold values from -0.046875 to 0.046875
- grad_basis: bfloat16 [16384, 16384], P('narrow', 'wide'), may hold values from -0.046875 to 0.046875
- eigenvalues: float32 [16384, 16384], P('wide', 'narrow'), may hold values from 0.1 to 10
- train_act: bfloat16 [64, 16384], P(None, 'narrow'), may hold values from -6 to 6
- train_grad: bfloat16 [64, 16384], P(None, 'wide'), may hold values from -6 to 6
Outputs:
- scores: float32 [64, 64], replicated
The draws below stay inside these ranges and needn't reach their ends.
All inputs are finite; a program needn't handle non-finite values.
Results may differ from the reference program's by a relative error of at most 0.0057.
Values may be sent and summed in bfloat16 or wider, within the bound.
No kernel may reach another device: no remote copies, remote signals or barrier semaphores. Data moves between devices by JAX's collectives and lax.ppermute only.
A program may use at most 128 MiB of HBM per device.

```python
import math
import jax
import jax.numpy as jnp
from jax import lax

A = 16384
G = 16384
Q = 64
TR = 64


def shard_levels(stream_key, extent, pieces, low, largest):
    level, own = 1.0, jax.random.fold_in(stream_key, 6)
    for axis_at, parts in pieces:
        heights = jnp.exp(jax.random.uniform(jax.random.fold_in(own, axis_at), (parts,), jnp.float32, low / len(pieces), largest / len(pieces)))
        level = level * jnp.repeat(heights, extent[axis_at] // parts).reshape([-1 if axis == axis_at else 1 for axis in range(len(extent))])
    return level


def scatter_about(key, dims, scale, bound, pieces=(), dtype=jnp.bfloat16):
    array = scale * jax.random.normal(key, dims, jnp.float32)
    if pieces:
        array = array * shard_levels(key, dims, pieces, -0.22, 0.18)
    return jnp.clip(array, -bound, bound).astype(dtype)


def setup_inputs(seed: int = 0) -> dict:
    keys = jax.random.split(jax.random.key(seed), 8)
    query_act = scatter_about(keys[0], (Q, A), 1.0, 6.0, ((1, 8),))
    query_grad = scatter_about(keys[1], (Q, G), 1.0, 6.0, ((1, 4),))
    act_basis = scatter_about(keys[2], (A, A), A ** -0.5, 0.046875, ((0, 8), (1, 4)))
    grad_basis = scatter_about(keys[3], (G, G), G ** -0.5, 0.046875, ((0, 4), (1, 8)))
    eigenvalues = jnp.clip(jnp.exp(math.log(10.0) - 4.6051702 * jax.random.uniform(keys[4], (G, A), jnp.float32) ** shard_levels(keys[4], (G, A), ((0, 8), (1, 4)), -0.2, 0.2)), 0.1, 10.0)
    train_act = scatter_about(keys[5], (TR, A), 1.0, 6.0, ((1, 4),))
    train_grad = scatter_about(keys[6], (TR, G), 1.0, 6.0, ((1, 8),))
    return {"query_act": query_act, "query_grad": query_grad, "act_basis": act_basis, "grad_basis": grad_basis, "eigenvalues": eigenvalues, "train_act": train_act, "train_grad": train_grad}


def reference(query_act, query_grad, act_basis, grad_basis, eigenvalues, train_act, train_grad):
    rot_act = jnp.dot(query_act, act_basis, preferred_element_type=jnp.float32).astype(jnp.bfloat16)
    rot_grad = jnp.dot(query_grad, grad_basis, preferred_element_type=jnp.float32).astype(jnp.bfloat16)
    inverse = lax.optimization_barrier((1.0 / eigenvalues).astype(jnp.bfloat16)).astype(jnp.float32)
    train_act32 = train_act.astype(jnp.float32)
    train_grad32 = train_grad.astype(jnp.float32)
    blocks_act = rot_act.reshape(Q // 8, 8, A)
    blocks_grad = rot_grad.reshape(Q // 8, 8, G)

    def one_block(items):
        block_act, block_grad = items
        pairs = (block_act.astype(jnp.float32)[:, None, :] * train_act32[None, :, :]).astype(jnp.bfloat16)
        pairs = lax.optimization_barrier(pairs).astype(jnp.float32)
        weighted = jnp.einsum("ij,btj->bti", inverse, pairs)
        factor = block_grad.astype(jnp.float32)[:, None, :] * train_grad32[None, :, :]
        return jnp.sum(weighted * factor, axis=2)

    totals = lax.map(one_block, (blocks_act, blocks_grad)).reshape(Q, TR)
    return totals * (float(A * G) ** -0.5)
```

```python
import jax
import jax.numpy as jnp
from jax import lax
from jax.experimental import pallas as pl
from jax.experimental.pallas import tpu as pltpu
from jax.sharding import PartitionSpec as P

BF16 = jnp.bfloat16
F32 = jnp.float32


def tile_of(extent, largest):
    return min(extent, largest)


def one_hot_rows(count, mask, dtype):
    rows = lax.broadcasted_iota(jnp.int32, (count, count), 0)
    cols = lax.broadcasted_iota(jnp.int32, (count, count), 1)
    return (cols == (rows ^ mask)).astype(F32).astype(dtype)


def rotate(mask, query, basis):
    count, inner = query.shape
    outer = basis.shape[1]
    step = tile_of(outer, max((1 << 20) // inner, 128))

    def kernel(mask_ref, query_ref, basis_ref, out_ref, mixed_ref):
        @pl.when(pl.program_id(0) == 0)
        def _():
            mixed_ref[...] = jnp.dot(
                one_hot_rows(count, mask_ref[0], BF16), query_ref[...], preferred_element_type=F32
            ).astype(BF16)

        out_ref[...] = jnp.dot(mixed_ref[...], basis_ref[...], preferred_element_type=F32)

    return pl.pallas_call(
        kernel,
        out_shape=jax.ShapeDtypeStruct((count, outer), F32),
        grid_spec=pltpu.PrefetchScalarGridSpec(
            num_scalar_prefetch=1,
            grid=(outer // step,),
            in_specs=[
                pl.BlockSpec((count, inner), lambda k, m: (0, 0)),
                pl.BlockSpec((inner, step), lambda k, m: (0, k)),
            ],
            out_specs=pl.BlockSpec((count, step), lambda k, m: (0, k)),
            scratch_shapes=[pltpu.VMEM((count, inner), BF16)],
        ),
        compiler_params=pltpu.CompilerParams(vmem_limit_bytes=40 << 20),
    )(mask, query, basis)


def contract(marks, act_own, act_other, grads, train_act, train_grad, eigenvalues):
    pieces = len(grads)
    rows_piece, inner = grads[0].shape
    count = rows_piece * pieces
    half = count // 2
    trains, outer = train_act.shape
    wide_tile = tile_of(outer, 512)
    tiles = outer // wide_tile
    chunk = min(16, count)
    chunks = count // chunk
    rows = chunk * trains

    def kernel(marks_ref, own_ref, other_ref, *refs):
        grad_refs = refs[:pieces]
        ta_ref, tg_ref, eig_ref, out_ref, f_ref, rg_ref, inv_ref, acc_ref = refs[pieces:]
        step = pl.program_id(0)
        core = marks_ref[0]

        def fill(m):
            tg = tg_ref[...]
            for r in range(chunk):
                g = rg_ref[pl.ds(m * chunk + r, 1), :]
                f_ref[m, pl.ds(r * trains, trains), :] = g * tg

        def work(filling):
            inv_ref[...] = (1.0 / eig_ref[...]).astype(BF16)
            ta = ta_ref[...].astype(F32)
            if filling:
                fill(0)
            for m in range(chunks):
                w = jnp.dot(f_ref[m], inv_ref[...], preferred_element_type=F32)
                if filling and m + 1 < chunks:
                    fill(m + 1)
                at = m * chunk
                first = at < half
                a_own = own_ref[pl.ds(at % half, chunk), :]
                a_other = other_ref[pl.ds(at % half, chunk), :]
                ra = jnp.where((core == 0) == first, a_own, a_other).astype(F32)
                p = (ra[:, None, :] * ta[None, :, :]).reshape(rows, wide_tile)
                w = w * p
                lanes = w[:, :128]
                for k in range(1, wide_tile // 128):
                    lanes = lanes + w[:, k * 128:(k + 1) * 128]
                if filling:
                    acc_ref[m] = lanes
                else:
                    acc_ref[m] += lanes

        @pl.when(step == 0)
        def _():
            for k in range(pieces):
                rg_ref[pl.ds(k * rows_piece, rows_piece), :] = grad_refs[k][...]
            work(True)

        @pl.when(step > 0)
        def _():
            work(False)

        @pl.when(step == tiles - 1)
        def _():
            total = jnp.sum(acc_ref[...].reshape(count, trains, 128), axis=-1)
            out_ref[...] = jnp.dot(
                one_hot_rows(count, marks_ref[1], F32), total,
                precision=lax.Precision.HIGHEST, preferred_element_type=F32,
            )

    whole = lambda shape: pl.BlockSpec(shape, lambda n, s: tuple(0 for _ in shape))
    return pl.pallas_call(
        kernel,
        out_shape=jax.ShapeDtypeStruct((count, trains), F32),
        grid_spec=pltpu.PrefetchScalarGridSpec(
            num_scalar_prefetch=1,
            grid=(tiles,),
            in_specs=[
                pl.BlockSpec((half, wide_tile), lambda n, s: (0, n)),
                pl.BlockSpec((half, wide_tile), lambda n, s: (0, n)),
                *[whole((rows_piece, inner)) for _ in range(pieces)],
                pl.BlockSpec((trains, wide_tile), lambda n, s: (0, n)),
                whole((trains, inner)),
                pl.BlockSpec((inner, wide_tile), lambda n, s: (0, n)),
            ],
            out_specs=whole((count, trains)),
            scratch_shapes=[
                pltpu.VMEM((chunks, rows, inner), BF16),
                pltpu.VMEM((count, inner), BF16),
                pltpu.VMEM((inner, wide_tile), BF16),
                pltpu.VMEM((chunks, rows, 128), F32),
            ],
        ),
        compiler_params=pltpu.CompilerParams(vmem_limit_bytes=60 << 20),
    )(marks, act_own, act_other, *grads, train_act, train_grad, eigenvalues)


def solution(mesh):
    wide, narrow = mesh.shape["wide"], mesh.shape["narrow"]

    def swap(value, axis, size, bit):
        return lax.ppermute(value, axis, [(i, i ^ bit) for i in range(size)])

    def bits(size, start=1):
        bit = start
        while bit < size:
            yield bit
            bit *= 2

    def on_device(query_act, query_grad, act_basis, grad_basis, eigenvalues, train_act, train_grad):
        count = query_act.shape[0]
        half, piece = count // 2, count // narrow
        core = lax.axis_index("wide") & 1
        row_mask = lax.axis_index("narrow") * piece
        act_mask = (row_mask ^ (core * half)).astype(jnp.int32).reshape(1)
        grad_mask = row_mask.astype(jnp.int32).reshape(1)
        marks = jnp.stack([core, row_mask]).astype(jnp.int32)

        part_act = rotate(act_mask, query_act, act_basis)
        sent = swap(part_act[half:].astype(BF16), "wide", wide, 1)
        part_grad = rotate(grad_mask, query_grad, grad_basis)
        act = part_act[:half] + sent.astype(F32)
        got = [
            swap(part_grad[k * piece:(k + 1) * piece].astype(BF16), "narrow", narrow, k)
            for k in range(1, narrow)
        ]
        for bit in bits(wide, 2):
            act = act + swap(act.astype(BF16), "wide", wide, bit).astype(F32)
        own = act.astype(BF16)
        other = swap(own, "wide", wide, 1)
        grad = part_grad[:piece]
        for value in got:
            grad = grad + value.astype(F32)
        grad = grad.astype(BF16)
        grads = [grad] + [swap(grad, "narrow", narrow, k) for k in range(1, narrow)]
        scores = contract(marks, own, other, grads, train_act, train_grad, eigenvalues)
        for bit in bits(wide):
            scores = scores + swap(scores, "wide", wide, bit)
        for bit in bits(narrow):
            scores = scores + swap(scores, "narrow", narrow, bit)
        inner, outer = eigenvalues.shape
        return scores * float(inner * wide * outer * narrow) ** (-0.5)

    in_specs = (
        P(None, "wide"),
        P(None, "narrow"),
        P("wide", "narrow"),
        P("narrow", "wide"),
        P("wide", "narrow"),
        P(None, "narrow"),
        P(None, "wide"),
    )
    return jax.shard_map(
        on_device, mesh=mesh, in_specs=in_specs, out_specs=P(), check_vma=False
    )
```

```python
import jax
import jax.numpy as jnp
from jax import lax
from jax.experimental import pallas as pl
from jax.experimental.pallas import tpu as pltpu
from jax.sharding import PartitionSpec as P


BF16 = jnp.bfloat16
F32 = jnp.float32


def tile_of(extent, largest):
    return min(extent, largest)


def one_hot_rows(count, mask, dtype):
    rows = lax.broadcasted_iota(jnp.int32, (count, count), 0)
    cols = lax.broadcasted_iota(jnp.int32, (count, count), 1)
    return (cols == (rows ^ mask)).astype(F32).astype(dtype)


def rotate(mask, query, basis, pieces):
    count, inner = query.shape
    outer = basis.shape[1]
    step = tile_of(outer, max((1 << 20) // inner, 128))
    steps = outer // step
    piece = count // pieces

    def kernel(mask_ref, query_hbm, basis_hbm, *refs):
        outs = refs[:pieces]
        query_ref, mixed_ref, basis_ref, query_sem, basis_sems = refs[pieces:]
        query_copy = pltpu.make_async_copy(query_hbm, query_ref, query_sem)
        query_copy.start()
        copies = [
            pltpu.make_async_copy(
                basis_hbm.at[:, pl.ds(k * step, step)], basis_ref.at[k], basis_sems.at[k]
            )
            for k in range(steps)
        ]
        for copy in copies:
            copy.start()
        query_copy.wait()
        mixed_ref[...] = jnp.dot(
            one_hot_rows(count, mask_ref[0], BF16), query_ref[...], preferred_element_type=F32
        ).astype(BF16)
        for k in range(steps):
            copies[k].wait()
            value = jnp.dot(mixed_ref[...], basis_ref[k], preferred_element_type=F32)
            for p in range(pieces):
                part = value[p * piece:(p + 1) * piece, :]
                outs[p][:, k * step:(k + 1) * step] = part.astype(outs[p].dtype)

    hbm = pl.BlockSpec(memory_space=pltpu.HBM)
    return pl.pallas_call(
        kernel,
        out_shape=[
            jax.ShapeDtypeStruct((piece, outer), BF16 if p else F32) for p in range(pieces)
        ],
        in_specs=[pl.BlockSpec(memory_space=pltpu.SMEM), hbm, hbm],
        out_specs=[pl.BlockSpec(memory_space=pltpu.VMEM) for _ in range(pieces)],
        scratch_shapes=[
            pltpu.VMEM((count, inner), BF16),
            pltpu.VMEM((count, inner), BF16),
            pltpu.VMEM((steps, inner, step), BF16),
            pltpu.SemaphoreType.DMA,
            pltpu.SemaphoreType.DMA((steps,)),
        ],
        compiler_params=pltpu.CompilerParams(vmem_limit_bytes=40 << 20),
        cost_estimate=pl.CostEstimate(
            flops=2 * count * inner * outer, transcendentals=0, bytes_accessed=2 * inner * outer
        ),
    )(mask, query, basis)


def contract(marks, act_own, act_other, grads, train_act, train_grad, eigenvalues):
    pieces = len(grads)
    rows_piece, inner = grads[0].shape
    count = rows_piece * pieces
    half = count // 2
    trains, outer = train_act.shape
    wide_tile = tile_of(outer, 512)
    tiles = outer // wide_tile
    chunk = min(16, count)
    chunks = count // chunk
    rows = chunk * trains

    def kernel(marks_ref, own_ref, other_ref, *refs):
        grad_refs = refs[:pieces]
        ta_ref, tg_ref, eig_ref, out_ref, f_ref, rg_ref, inv_ref, acc_ref = refs[pieces:]
        step = pl.program_id(0)
        core = marks_ref[0]

        def fill(m):
            tg = tg_ref[...]
            for r in range(chunk):
                g = rg_ref[pl.ds(m * chunk + r, 1), :]
                f_ref[m, pl.ds(r * trains, trains), :] = g * tg

        def work(filling):
            inv_ref[...] = (1.0 / eig_ref[...]).astype(BF16)
            ta = ta_ref[...].astype(F32)
            if filling:
                fill(0)
            for m in range(chunks):
                w = jnp.dot(f_ref[m], inv_ref[...], preferred_element_type=F32)
                if filling and m + 1 < chunks:
                    fill(m + 1)
                at = m * chunk
                first = at < half
                a_own = own_ref[pl.ds(at % half, chunk), :]
                a_other = other_ref[pl.ds(at % half, chunk), :]
                ra = jnp.where((core == 0) == first, a_own, a_other).astype(F32)
                p = (ra[:, None, :] * ta[None, :, :]).reshape(rows, wide_tile)
                w = w * p
                lanes = w[:, :128]
                for k in range(1, wide_tile // 128):
                    lanes = lanes + w[:, k * 128:(k + 1) * 128]
                if filling:
                    acc_ref[m] = lanes
                else:
                    acc_ref[m] += lanes

        @pl.when(step == 0)
        def _():
            for k in range(pieces):
                rg_ref[pl.ds(k * rows_piece, rows_piece), :] = grad_refs[k][...]
            work(True)

        @pl.when(step > 0)
        def _():
            work(False)

        @pl.when(step == tiles - 1)
        def _():
            total = jnp.sum(acc_ref[...].reshape(count, trains, 128), axis=-1)
            out_ref[...] = jnp.dot(
                one_hot_rows(count, marks_ref[1], F32), total,
                precision=lax.Precision.HIGHEST, preferred_element_type=F32,
            )

    whole = lambda shape: pl.BlockSpec(shape, lambda n, s: tuple(0 for _ in shape))
    return pl.pallas_call(
        kernel,
        out_shape=jax.ShapeDtypeStruct((count, trains), F32),
        grid_spec=pltpu.PrefetchScalarGridSpec(
            num_scalar_prefetch=1,
            grid=(tiles,),
            in_specs=[
                pl.BlockSpec((half, wide_tile), lambda n, s: (0, n)),
                pl.BlockSpec((half, wide_tile), lambda n, s: (0, n)),
                *[whole((rows_piece, inner)) for _ in range(pieces)],
                pl.BlockSpec((trains, wide_tile), lambda n, s: (0, n)),
                whole((trains, inner)),
                pl.BlockSpec((inner, wide_tile), lambda n, s: (0, n)),
            ],
            out_specs=whole((count, trains)),
            scratch_shapes=[
                pltpu.VMEM((chunks, rows, inner), BF16),
                pltpu.VMEM((count, inner), BF16),
                pltpu.VMEM((inner, wide_tile), BF16),
                pltpu.VMEM((chunks, rows, 128), F32),
            ],
        ),
        compiler_params=pltpu.CompilerParams(vmem_limit_bytes=44 << 20),
    )(marks, act_own, act_other, *grads, train_act, train_grad, eigenvalues)


def solution(mesh):
    wide, narrow = mesh.shape["wide"], mesh.shape["narrow"]

    def swap(value, axis, size, bit):
        return lax.ppermute(value, axis, [(i, i ^ bit) for i in range(size)])

    def bits(size, start=1):
        bit = start
        while bit < size:
            yield bit
            bit *= 2

    def whole_step(query_act, query_grad, act_basis, grad_basis, eigenvalues, train_act, train_grad):
        count = query_act.shape[0]
        half, piece = count // 2, count // narrow
        core = lax.axis_index("wide") & 1
        row_mask = lax.axis_index("narrow") * piece
        act_mask = (row_mask ^ (core * half)).astype(jnp.int32).reshape(1)
        grad_mask = row_mask.astype(jnp.int32).reshape(1)
        marks = jnp.stack([core, row_mask]).astype(jnp.int32)

        grad, *leaving = rotate(grad_mask, query_grad, grad_basis, narrow)
        got = [swap(leaving[k - 1], "narrow", narrow, k) for k in range(1, narrow)]
        act, leaving = rotate(act_mask, query_act, act_basis, 2)
        paired = swap(leaving, "wide", wide, 1)
        for value in got:
            grad = grad + value.astype(F32)
        grad = grad.astype(BF16)
        grads = [grad] + [swap(grad, "narrow", narrow, k) for k in range(1, narrow)]
        act = act + paired.astype(F32)
        middle = act.shape[1] // 2
        left, right = act[:, :middle], act[:, middle:]
        order = list(bits(wide, 2))
        for bit_left, bit_right in zip(order, reversed(order)):
            from_left = swap(left.astype(BF16), "wide", wide, bit_left)
            from_right = swap(right.astype(BF16), "wide", wide, bit_right)
            left = left + from_left.astype(F32)
            right = right + from_right.astype(F32)
        own = jnp.concatenate([left.astype(BF16), right.astype(BF16)], axis=1)
        other = swap(own, "wide", wide, 1)
        scores = contract(marks, own, other, grads, train_act, train_grad, eigenvalues)
        for bit in bits(wide):
            scores = scores + swap(scores, "wide", wide, bit)
        for bit in bits(narrow):
            scores = scores + swap(scores, "narrow", narrow, bit)
        inner, outer = eigenvalues.shape
        return scores * float(inner * wide * outer * narrow) ** (-0.5)

    in_specs = (
        P(None, "wide"),
        P(None, "narrow"),
        P("wide", "narrow"),
        P("narrow", "wide"),
        P("wide", "narrow"),
        P(None, "narrow"),
        P(None, "wide"),
    )
    return jax.shard_map(whole_step, mesh=mesh, in_specs=in_specs, out_specs=P(), check_vma=False)
```

```python
import jax
import jax.numpy as jnp
from jax import lax
from jax.experimental import pallas as pl
from jax.experimental.pallas import tpu as pltpu
from jax.sharding import PartitionSpec as P


BF16 = jnp.bfloat16
F32 = jnp.float32


def tile_of(extent, largest):
    return min(extent, largest)


def one_hot_rows(count, mask, dtype):
    rows = lax.broadcasted_iota(jnp.int32, (count, count), 0)
    cols = lax.broadcasted_iota(jnp.int32, (count, count), 1)
    return (cols == (rows ^ mask)).astype(F32).astype(dtype)


def rotate(mask, query, basis, pieces):
    count, inner = query.shape
    outer = basis.shape[1]
    deep = tile_of(inner, 2048)
    step = tile_of(outer, max((1 << 20) // deep, 128))
    steps, depths = outer // step, inner // deep
    piece = count // pieces

    def kernel(mask_ref, query_hbm, basis_hbm, *refs):
        outs = refs[:pieces]
        query_ref, mixed_ref, basis_ref, query_sem, basis_sems = refs[pieces:]
        query_copy = pltpu.make_async_copy(query_hbm, query_ref, query_sem)
        query_copy.start()
        copies = [
            [
                pltpu.make_async_copy(
                    basis_hbm.at[pl.ds(d * deep, deep), pl.ds(k * step, step)],
                    basis_ref.at[k, d],
                    basis_sems.at[k, d],
                )
                for d in range(depths)
            ]
            for k in range(steps)
        ]
        for row in copies:
            for copy in row:
                copy.start()
        query_copy.wait()
        mixed_ref[...] = jnp.dot(
            one_hot_rows(count, mask_ref[0], BF16), query_ref[...], preferred_element_type=F32
        ).astype(BF16)
        for k in range(steps):
            value = jnp.zeros((count, step), F32)
            for d in range(depths):
                copies[k][d].wait()
                value = value + jnp.dot(
                    mixed_ref[:, d * deep:(d + 1) * deep], basis_ref[k, d],
                    preferred_element_type=F32,
                )
            for p in range(pieces):
                part = value[p * piece:(p + 1) * piece, :]
                outs[p][:, k * step:(k + 1) * step] = part.astype(outs[p].dtype)

    hbm = pl.BlockSpec(memory_space=pltpu.HBM)
    return pl.pallas_call(
        kernel,
        out_shape=[
            jax.ShapeDtypeStruct((piece, outer), BF16 if p else F32) for p in range(pieces)
        ],
        in_specs=[pl.BlockSpec(memory_space=pltpu.SMEM), hbm, hbm],
        out_specs=[pl.BlockSpec(memory_space=pltpu.VMEM) for _ in range(pieces)],
        scratch_shapes=[
            pltpu.VMEM((count, inner), BF16),
            pltpu.VMEM((count, inner), BF16),
            pltpu.VMEM((steps, depths, deep, step), BF16),
            pltpu.SemaphoreType.DMA,
            pltpu.SemaphoreType.DMA((steps, depths)),
        ],
        compiler_params=pltpu.CompilerParams(vmem_limit_bytes=40 << 20),
        cost_estimate=pl.CostEstimate(
            flops=2 * count * inner * outer, transcendentals=0, bytes_accessed=2 * inner * outer
        ),
    )(mask, pltpu.with_memory_space_constraint(query, pltpu.HBM), basis)


def prepare(eigenvalues):
    inner, outer = eigenvalues.shape
    wide_tile = tile_of(outer, 1024)
    parts = 4
    part = wide_tile // parts

    def kernel(eig_hbm, out_ref, eig_ref, sems):
        copies = [
            pltpu.make_async_copy(
                eig_hbm.at[:, pl.ds(k * part, part)], eig_ref.at[k], sems.at[k]
            )
            for k in range(parts)
        ]
        for copy in copies:
            copy.start()
        for k in range(parts):
            copies[k].wait()
            out_ref[:, k * part:(k + 1) * part] = (1.0 / eig_ref[k]).astype(BF16)

    return pl.pallas_call(
        kernel,
        out_shape=jax.ShapeDtypeStruct((inner, wide_tile), BF16),
        in_specs=[pl.BlockSpec(memory_space=pltpu.HBM)],
        out_specs=pl.BlockSpec(memory_space=pltpu.VMEM),
        scratch_shapes=[
            pltpu.VMEM((parts, inner, part), F32),
            pltpu.SemaphoreType.DMA((parts,)),
        ],
        compiler_params=pltpu.CompilerParams(vmem_limit_bytes=24 << 20),
        cost_estimate=pl.CostEstimate(
            flops=inner * wide_tile, transcendentals=0, bytes_accessed=6 * inner * wide_tile
        ),
    )(eigenvalues)


def contract(marks, act_own, act_other, grads, train_act, train_grad, first_inverse, eigenvalues):
    pieces = len(grads)
    rows_piece, inner = grads[0].shape
    count = rows_piece * pieces
    half = count // 2
    trains, outer = train_act.shape
    wide_tile = tile_of(outer, 1024)
    tiles = outer // wide_tile
    chunk = min(16, count)
    chunks = count // chunk
    rows = chunk * trains

    def kernel(marks_ref, own_ref, other_ref, *refs):
        grad_refs = refs[:pieces]
        ta_ref, tg_ref, first_ref, eig_hbm, out_ref = refs[pieces:pieces + 5]
        f_ref, rg_ref, inv_ref, acc_ref, eig_ref, eig_sems = refs[pieces + 5:]
        step = pl.program_id(0)
        core = marks_ref[0]

        def fill(m):
            tg = tg_ref[...]
            for r in range(chunk):
                g = rg_ref[pl.ds(m * chunk + r, 1), :]
                f_ref[m, pl.ds(r * trains, trains), :] = g * tg

        def fetch(tile):
            return pltpu.make_async_copy(
                eig_hbm.at[:, pl.ds(pl.multiple_of(tile * wide_tile, wide_tile), wide_tile)],
                eig_ref.at[tile % 2],
                eig_sems.at[tile % 2],
            )

        def work(filling):
            inverse_ref = first_ref if filling else inv_ref
            if not filling:
                inv_ref[...] = (1.0 / eig_ref[step % 2]).astype(BF16)
            ta = ta_ref[...].astype(F32)
            if filling:
                fill(0)
            for m in range(chunks):
                w = jnp.dot(f_ref[m], inverse_ref[...], preferred_element_type=F32)
                if filling and m + 1 < chunks:
                    fill(m + 1)
                at = m * chunk
                first = at < half
                a_own = own_ref[pl.ds(at % half, chunk), :]
                a_other = other_ref[pl.ds(at % half, chunk), :]
                ra = jnp.where((core == 0) == first, a_own, a_other).astype(F32)
                p = (ra[:, None, :] * ta[None, :, :]).reshape(rows, wide_tile)
                w = w * p
                lanes = w[:, :128]
                for k in range(1, wide_tile // 128):
                    lanes = lanes + w[:, k * 128:(k + 1) * 128]
                if filling:
                    acc_ref[m] = lanes
                else:
                    acc_ref[m] += lanes

        @pl.when(step == 0)
        def _():
            if tiles > 1:
                fetch(1).start()
            for k in range(pieces):
                rg_ref[pl.ds(k * rows_piece, rows_piece), :] = grad_refs[k][...]
            work(True)

        if tiles > 1:

            @pl.when(step > 0)
            def _():
                fetch(step).wait()

                @pl.when(step + 1 < tiles)
                def _():
                    fetch(step + 1).start()

                work(False)

        @pl.when(step == tiles - 1)
        def _():
            total = jnp.sum(acc_ref[...].reshape(count, trains, 128), axis=-1)
            out_ref[...] = jnp.dot(
                one_hot_rows(count, marks_ref[1], F32), total,
                precision=lax.Precision.HIGHEST, preferred_element_type=F32,
            )

    whole = lambda shape: pl.BlockSpec(
        shape, lambda n, s: tuple(0 for _ in shape), pipeline_mode=pl.Buffered(1)
    )
    return pl.pallas_call(
        kernel,
        out_shape=jax.ShapeDtypeStruct((count, trains), F32),
        grid_spec=pltpu.PrefetchScalarGridSpec(
            num_scalar_prefetch=1,
            grid=(tiles,),
            in_specs=[
                pl.BlockSpec((half, wide_tile), lambda n, s: (0, n)),
                pl.BlockSpec((half, wide_tile), lambda n, s: (0, n)),
                *[whole((rows_piece, inner)) for _ in range(pieces)],
                pl.BlockSpec((trains, wide_tile), lambda n, s: (0, n)),
                whole((trains, inner)),
                whole((inner, wide_tile)),
                pl.BlockSpec(memory_space=pltpu.HBM),
            ],
            out_specs=pl.BlockSpec((count, trains), lambda n, s: (0, 0)),
            scratch_shapes=[
                pltpu.VMEM((chunks, rows, inner), BF16),
                pltpu.VMEM((count, inner), BF16),
                pltpu.VMEM((inner, wide_tile), BF16),
                pltpu.VMEM((chunks, rows, 128), F32),
                pltpu.VMEM((2, inner, wide_tile), F32),
                pltpu.SemaphoreType.DMA((2,)),
            ],
        ),
        compiler_params=pltpu.CompilerParams(vmem_limit_bytes=49 << 20),
    )(marks, act_own, act_other, *grads, train_act, train_grad, first_inverse, eigenvalues)


def solution(mesh):
    wide, narrow = mesh.shape["wide"], mesh.shape["narrow"]

    def swap(value, axis, size, bit):
        return lax.ppermute(value, axis, [(i, i ^ bit) for i in range(size)])

    def bits(size, start=1):
        bit = start
        while bit < size:
            yield bit
            bit *= 2

    def whole_step(query_act, query_grad, act_basis, grad_basis, eigenvalues, train_act, train_grad):
        count = query_act.shape[0]
        half, piece = count // 2, count // narrow
        core = lax.axis_index("wide") & 1
        row_mask = lax.axis_index("narrow") * piece
        act_mask = (row_mask ^ (core * half)).astype(jnp.int32).reshape(1)
        grad_mask = row_mask.astype(jnp.int32).reshape(1)
        marks = jnp.stack([core, row_mask]).astype(jnp.int32)

        grad, *leaving = rotate(grad_mask, query_grad, grad_basis, narrow)
        got = [swap(leaving[k - 1], "narrow", narrow, k) for k in range(1, narrow)]
        act, leaving = rotate(act_mask, query_act, act_basis, 2)
        paired = swap(leaving, "wide", wide, 1)
        for value in got:
            grad = grad + value.astype(F32)
        grad = grad.astype(BF16)
        grads = [grad] + [swap(grad, "narrow", narrow, k) for k in range(1, narrow)]
        act = act + paired.astype(F32)
        middle = act.shape[1] // 2
        left, right = act[:, :middle], act[:, middle:]
        order = list(bits(wide, 2))
        first_inverse = prepare(eigenvalues)
        for bit_left, bit_right in zip(order, reversed(order)):
            from_left = swap(left.astype(BF16), "wide", wide, bit_left)
            from_right = swap(right.astype(BF16), "wide", wide, bit_right)
            left = left + from_left.astype(F32)
            right = right + from_right.astype(F32)
        own = jnp.concatenate([left.astype(BF16), right.astype(BF16)], axis=1)
        other = swap(own, "wide", wide, 1)
        scores = contract(
            marks, own, other, grads, train_act, train_grad, first_inverse, eigenvalues
        )
        for bit in bits(wide):
            scores = scores + swap(scores, "wide", wide, bit)
        for bit in bits(narrow):
            scores = scores + swap(scores, "narrow", narrow, bit)
        inner, outer = eigenvalues.shape
        return scores * float(inner * wide * outer * narrow) ** (-0.5)

    in_specs = (
        P(None, "wide"),
        P(None, "narrow"),
        P("wide", "narrow"),
        P("narrow", "wide"),
        P("wide", "narrow"),
        P(None, "narrow"),
        P(None, "wide"),
    )
    return jax.shard_map(whole_step, mesh=mesh, in_specs=in_specs, out_specs=P(), check_vma=False)
```
